256 devices in a mesh: col: 32 (over x, y, core), row: 8 (over z).
Axes of the slice: x: 4, y: 4, z: 8, core: 2. Of those that a mesh axis runs over, the one named last changes fastest.
Arguments:
- weights: float32 [4096, 53248], P('row', 'col'), may hold values from -6 to 6
- factor: float32 [6, 512, 53248], P(None, 'row', 'col'), as said below
- diag_inverse: float32 [6, 4, 128, 128], replicated
- prune_mask: int32 [6, 32, 4], P(None, 'row'), may hold values 0 or 1
- panel_start: int32 [6], replicated, may hold values from 0 to 52736, as said below
Outputs:
- pruned: float32 [4096, 53248], P('row', 'col')
The draws below stay inside these ranges and needn't reach their ends.
Inputs may be any that keep to these rules, and one draw needn't show every extreme that they name: `panel_start`: strictly increasing; each a multiple of 128; each panel lies within one block of 1664 columns, and no two panels in the same block. `factor`: row j of panel k is zero left of column panel_start[k] + j and positive on it.
All inputs are finite; a program needn't handle non-finite values. No bound on the sum of `prune_mask` on one device may be relied on, other than what follows from the above.
Results may differ from the reference program's by a relative error of at most 0.0001.
Values sent between devices are 32-bit elements; how exact they have to be, the bound alone decides.
No kernel may reach another device: no remote copies, remote signals or barrier semaphores. Data moves between devices by JAX's collectives and lax.ppermute only.
A program may use at most 192 MiB of HBM per device.

```python
import jax
import jax.numpy as jnp
from jax import lax

C = 53248
TILE = 128
PANEL_TILES = 4
PW = 512
P_SIZE = 6
ROWS = 4096
CDEV = 1664
N_COL = 32


def panel_starts(key):
    middle = jax.random.permutation(jax.random.fold_in(key, 11), N_COL - 2)[:P_SIZE - 2] + 1
    owners = jnp.sort(jnp.concatenate([jnp.zeros((1,), jnp.int32), middle.astype(jnp.int32), jnp.full((1,), N_COL - 1, jnp.int32)]))
    offsets = jax.random.randint(jax.random.fold_in(key, 12), (P_SIZE,), 0, CDEV // TILE - PANEL_TILES + 1).astype(jnp.int32)
    offsets = offsets.at[0].set(0).at[P_SIZE - 1].set(CDEV // TILE - PANEL_TILES)
    return (owners * CDEV + offsets * TILE).astype(jnp.int32)


def factor_pair(key):
    starts = panel_starts(key)
    noise = jax.random.normal(jax.random.fold_in(key, 21), (P_SIZE, PW, C), jnp.float32)
    diag = jnp.exp(jax.random.uniform(jax.random.fold_in(key, 23), (P_SIZE, PW), jnp.float32, -0.36, 0.34))
    position = starts[:, None] + jnp.arange(PW, dtype=jnp.int32)[None, :]
    offset = jnp.arange(C, dtype=jnp.int32)[None, None, :] - position[:, :, None]
    factor = jnp.where(offset > 0, 0.03 * noise, 0.0) + jnp.where(offset == 0, diag[:, :, None], 0.0)
    blocks = jax.vmap(lambda rows, first: lax.dynamic_slice(rows, (0, first), (PW, PW)))(factor, starts)
    tiles = jnp.stack([blocks[:, a * TILE:(a + 1) * TILE, a * TILE:(a + 1) * TILE] for a in range(PANEL_TILES)], 1)
    identity = jnp.broadcast_to(jnp.eye(TILE, dtype=jnp.float32), tiles.shape)
    inverse = lax.linalg.triangular_solve(tiles, identity, left_side=True, lower=False)
    return (factor, inverse)


def draw_panel_start(key, part):
    return panel_starts(key)


def draw_factor(key, part):
    return factor_pair(key)[0]


def draw_diag_inverse(key, part):
    return factor_pair(key)[1]


def plant(values, key, smallest, largest):
    longest = values.shape.index(max(values.shape))
    spots = []
    for shift in (0, 1):
        where = [jax.random.randint(jax.random.fold_in(key, axis), (), 0, length) for axis, length in enumerate(values.shape)]
        where[longest] = (where[longest] + shift) % values.shape[longest]
        spots.append(tuple(where))
    return values.at[spots[0]].set(smallest).at[spots[1]].set(largest)


def shard_levels(own_key, dims, pieces, smallest, high):
    def one(dim, shards_of):
        heights = jax.random.uniform(jax.random.fold_in(jax.random.fold_in(own_key, 6), dim), (shards_of,), jnp.float32, smallest / len(pieces), high / len(pieces))
        return jnp.repeat(jnp.exp(heights), dims[dim] // shards_of).reshape((-1,) + (1,) * (len(dims) - dim - 1))

    level = one(*pieces[0])
    for cut in pieces[1:]:
        level = level * one(*cut)
    return level


def centred(stream_key, extent, scale, bound, split=(), kind=jnp.bfloat16):
    drawn = scale * jax.random.normal(stream_key, extent, jnp.float32)
    if split:
        drawn = drawn * shard_levels(stream_key, extent, split, -0.22, 0.18)
    return jnp.clip(drawn, -bound, bound).astype(kind)


def setup_inputs(seed: int = 0) -> dict:
    arg_keys = jax.random.split(jax.random.key(seed), 6)
    return {
        "weights": centred(arg_keys[0], (ROWS, C), 1.0, 6.0, ((0, 8), (1, 32)), jnp.float32),
        "factor": draw_factor(jax.random.fold_in(arg_keys[5], 71), 0),
        "diag_inverse": draw_diag_inverse(jax.random.fold_in(arg_keys[5], 71), 0),
        "prune_mask": plant((jax.random.randint(arg_keys[3], (P_SIZE, ROWS // TILE, PANEL_TILES), 0, 2) < 1).astype(jnp.int32), jax.random.fold_in(arg_keys[3], 1), 0, 1),
        "panel_start": draw_panel_start(jax.random.fold_in(arg_keys[5], 71), 0),
    }


def panel_errors(wpanel, ublock, dinv, rowmask):
    tiles = []
    for a in range(PANEL_TILES):
        acc = wpanel[:, a * TILE:(a + 1) * TILE]
        for b in range(a):
            acc = acc - jnp.dot(tiles[b], ublock[b * TILE:(b + 1) * TILE, a * TILE:(a + 1) * TILE], precision=lax.Precision.HIGHEST)
        tiles.append(rowmask[:, a:a + 1] * jnp.dot(acc, dinv[a], precision=lax.Precision.HIGHEST))
    return jnp.concatenate(tiles, 1)

def reference(weights, factor, diag_inverse, prune_mask, panel_start):
    zero = jnp.zeros((), jnp.int32)
    starts = TILE * jnp.arange(PANEL_TILES, dtype=jnp.int32)
    for k in range(P_SIZE):
        first = panel_start[k].astype(jnp.int32)
        rows_k = factor[k]
        ublock = lax.dynamic_slice(rows_k, (zero, first), (PW, PW))
        wpanel = lax.dynamic_slice(weights, (zero, first), (ROWS, PW))
        rowmask = jnp.repeat(prune_mask[k].astype(jnp.float32), TILE, axis=0)
        errors = panel_errors(wpanel, ublock, diag_inverse[k], rowmask)
        weights = weights - jnp.dot(errors, rows_k, precision=lax.Precision.HIGHEST)
        offset = jnp.arange(C, dtype=jnp.int32) - first
        indicator = ((offset[None, :] >= starts[:, None]) & (offset[None, :] < starts[:, None] + TILE)).astype(jnp.float32)
        prune = jnp.dot(rowmask, indicator, precision=lax.Precision.HIGHEST)
        weights = weights * (1.0 - prune)
    return weights
```

```python
import functools

import jax
import jax.numpy as jnp
import numpy as np
from jax import lax
from jax.experimental import pallas as pl
from jax.experimental.pallas import tpu as pltpu
from jax.sharding import Mesh
from jax.sharding import PartitionSpec as P

TILE = 128
PANEL_TILES = 4
PW = 512
P_SIZE = 6
N_COL = 32
COL = ("col_0", "col_1", "col_2")
HOPS = ((0, 1), (1, 1), (0, 3), (1, 3))
BLOCKS = [(k, m) for k in range(P_SIZE) for m in range(k + 1)]
SLOTS = 6
HALF = SLOTS // 2
MINE = 16
NARROW = 256


def device(x, y, core):
    return (x * 4 + y) * 2 + core


def exchange(stream, stage):
    pairs = []
    for x in range(4):
        for y in range(4):
            for core in range(2):
                axis, bits = HOPS[(stream + stage + 2 * core) % 4]
                there = (x ^ bits, y) if axis == 0 else (x, y ^ bits)
                pairs.append((device(x, y, core), device(*there, core)))
    return pairs


def other_core(value):
    return lax.ppermute(value, "col_2", [(0, 1), (1, 0)])


def spread(streams):
    near = [value[None] for value in streams]
    for stage in range(3):
        near = [
            jnp.concatenate([value, lax.ppermute(value, COL, exchange(i, stage))], 0)
            for i, value in enumerate(near)
        ]
    far = [lax.ppermute(value, COL, exchange(i, 3)) for i, value in enumerate(near)]
    return [
        [near[i], far[i], other_core(near[i]), other_core(far[i])] for i in range(len(streams))
    ]


def all_rows(value):
    height = lax.axis_size("row")
    up = [(z, (z + 1) % height) for z in range(height)]
    down = [(z, (z - 1) % height) for z in range(height)]
    below, above = [value], [value]
    for hop in range(height // 2):
        below.append(lax.ppermute(below[-1], "row", up))
        if hop < height // 2 - 1:
            above.append(lax.ppermute(above[-1], "row", down))
    here = lax.axis_index("row")
    whole = jnp.zeros((value.shape[0], height, *value.shape[1:]), value.dtype)
    for i, part in enumerate(above + below[:0:-1]):
        place = lax.rem(here + i, height)
        whole = lax.dynamic_update_slice_in_dim(whole, part[:, None], place, 1)
    return whole


def sources():
    x, y, own = (lax.axis_index(name) for name in COL)
    steps = []
    for axis in range(2):
        value = np.zeros((2, 2, 16), np.int32)
        for core in range(2):
            for stream in range(2):
                for unit in range(16):
                    for stage in range(4):
                        hop, bits = HOPS[(stream + stage + 2 * core) % 4]
                        if hop == axis and unit >> stage & 1:
                            value[core, stream, unit] ^= bits
        steps.append(jnp.asarray(value))
    rows = []
    for core in (own, 1 - own):
        there_x = x ^ jnp.where(core == 0, steps[0][0], steps[0][1])
        there_y = y ^ jnp.where(core == 0, steps[1][0], steps[1][1])
        rows.append(device(there_x, there_y, core))
    return jnp.stack(rows, 1).astype(jnp.int32).reshape(-1)


def halves(value):
    high = value.astype(jnp.bfloat16)
    low = (value - high.astype(jnp.float32)).astype(jnp.bfloat16)
    return high, low


def product(left, right):
    dot = functools.partial(jnp.dot, preferred_element_type=jnp.float32)
    return dot(left[0], right[0]) + (dot(left[0], right[1]) + dot(left[1], right[0]))


def unit_copies(refs, place, semaphores):
    copies = []
    for stream in range(2):
        group = []
        for part in range(4):
            for unit in range(8):
                number = (stream * 2 + part // 2) * 16 + part % 2 * 8 + unit
                group.append(
                    pltpu.make_async_copy(
                        refs[stream * 4 + part].at[unit],
                        place(stream, number),
                        semaphores.at[number],
                    )
                )
        copies.append(group)
    return copies


def solve_kernel(source, flags, *refs):
    parts, (windows, inverse), outs = refs[:8], refs[8:10], refs[10:12]
    blocks, errors, semaphores = refs[12:]

    def place(stream, number):
        place_of = source[number]
        return blocks.at[pl.ds(stream * HALF, HALF), place_of // 8, :, lax.rem(place_of, 8)]

    copies = unit_copies(parts, place, semaphores)
    for group in copies:
        for copy in group:
            copy.start()
    for copy in copies[0]:
        copy.wait()
    arrived = 1

    def block_at(number):
        return halves(blocks[number // 4, lax.rem(number, 4)].reshape(PW, PW))

    for k in range(P_SIZE):
        base = k * (k + 1) // 2
        if base + k >= 4 * HALF and arrived == 1:
            for copy in copies[1]:
                copy.wait()
            arrived = 2

        def take(m, acc, base=base):
            return acc - product((errors[m, 0], errors[m, 1]), block_at(base + m))

        window = lax.fori_loop(0, k, take, windows[k])
        block = block_at(base + k)
        done = []
        for a in range(PANEL_TILES):
            tile = slice(a * TILE, (a + 1) * TILE)
            acc = window[:, tile]
            if a:
                left = tuple(jnp.concatenate([d[i] for d in done], 1) for i in range(2))
                acc = acc - product(left, tuple(b[: a * TILE, tile] for b in block))
            acc = product(halves(acc), halves(inverse[k, a]))
            acc = jnp.where(flags[k, a] != 0, acc, 0.0)
            done.append(halves(acc))
            column = (k % 3) * PW + a * TILE
            outs[k // 3][:, column : column + TILE] = acc
        for i in range(2):
            errors[k, i] = jnp.concatenate([d[i] for d in done], 1)


def assemble_kernel(source, *refs):
    parts, (out, errors, semaphores) = refs[:8], refs[8:]

    def place(stream, number):
        first = pl.multiple_of(source[number] * MINE, MINE)
        return errors.at[stream, pl.ds(first, MINE)]

    copies = unit_copies(parts, place, semaphores)
    for group in copies:
        for copy in group:
            copy.start()
    for stream, group in enumerate(copies):
        for copy in group:
            copy.wait()
        for k in range(3 * stream, 3 * stream + 3):
            high, low = halves(errors[stream, :, (k % 3) * PW : (k % 3 + 1) * PW])
            out[k, :, :PW] = high
            out[k, :, PW : 2 * PW] = low
            out[k, :, 2 * PW :] = high


def update_kernel(flags, errors, weights, factor, out):
    n = pl.program_id(0)
    out[...] = weights[...]

    def take(k, carry):
        high, low = halves(factor[k])
        rows = jnp.concatenate([high, high, low], 0)
        out[...] = out[...] - jnp.dot(errors[k], rows, preferred_element_type=jnp.float32)
        return carry

    lax.fori_loop(0, P_SIZE, take, 0)
    for part in range(NARROW // TILE):
        tile = n * (NARROW // TILE) + part - flags[0]
        inside = jnp.logical_and(tile >= 0, tile < PANEL_TILES)
        a = jnp.clip(tile, 0, PANEL_TILES - 1)
        columns = slice(part * TILE, (part + 1) * TILE)
        for r in range(4):
            gone = jnp.logical_and(inside, flags[1 + r * PANEL_TILES + a] != 0)

            @pl.when(gone)
            def _(r=r, columns=columns):
                out[r * TILE : (r + 1) * TILE, columns] = jnp.zeros((TILE, TILE), jnp.float32)


def shards(weights, factor, diag_inverse, prune_mask, panel_start):
    rows, width = weights.shape
    slab = factor.shape[1]
    me = lax.axis_index(COL)
    owner = panel_start // width
    mine = owner == me
    shift = jnp.sum(jnp.where(mine, panel_start - me * width, 0))
    panel = jnp.sum(jnp.where(mine, jnp.arange(P_SIZE, dtype=jnp.int32), 0))
    gathered = lax.all_gather(factor, "row", axis=1, tiled=True)

    window = lax.dynamic_slice(factor, (0, 0, shift), (P_SIZE, slab, PW))
    window = window.reshape(P_SIZE, 8, 8, PW)
    turn = lax.rem(panel * (panel + 1) // 2, 4)
    order = lax.rem(jnp.arange(4, dtype=jnp.int32) + 4 - turn, 4)
    order = jnp.minimum(order[:, None] + jnp.array([0, 4], jnp.int32), P_SIZE - 1)
    eighths = jnp.swapaxes(window[order], 1, 2).reshape(N_COL, 16, PW)
    wanted = lax.dynamic_slice(weights, (0, shift), (rows, PW)).reshape(N_COL, MINE, PW)
    arrived = lax.all_to_all(
        jnp.concatenate([eighths, wanted], 1), COL, 0, 0, tiled=True
    ).reshape(4 * N_COL, 8, PW)

    numbers = jnp.minimum(4 * jnp.arange(SLOTS, dtype=jnp.int32) + me // 8, len(BLOCKS) - 1)
    panels = jnp.array([k for k, _ in BLOCKS], jnp.int32)[numbers]
    parts = jnp.array([m // 4 for _, m in BLOCKS], jnp.int32)[numbers]
    picked = all_rows(arrived[owner[panels] * 4 + parts])
    windows = arrived[(owner[:, None] * 4 + jnp.array([2, 3], jnp.int32)).reshape(-1)]
    windows = windows.reshape(P_SIZE, MINE, PW)
    source = sources()
    spread_parts = spread([picked[:HALF], picked[HALF:]])

    own_rows = lax.dynamic_slice(prune_mask, (0, me // 8, 0), (P_SIZE, 1, PANEL_TILES))[:, 0]
    any_spec = pl.BlockSpec(memory_space=pl.ANY)
    vmem = pl.BlockSpec(memory_space=pltpu.VMEM)
    smem = pl.BlockSpec(memory_space=pltpu.SMEM)
    found = pl.pallas_call(
        solve_kernel,
        out_shape=[jax.ShapeDtypeStruct((MINE, 3 * PW), jnp.float32)] * 2,
        in_specs=[smem, smem] + [any_spec] * 8 + [vmem, vmem],
        out_specs=[vmem, vmem],
        scratch_shapes=[
            pltpu.VMEM((SLOTS, 4, 8, 8, 8, PW), jnp.float32),
            pltpu.VMEM((P_SIZE, 2, MINE, PW), jnp.bfloat16),
            pltpu.SemaphoreType.DMA((64,)),
        ],
        compiler_params=pltpu.CompilerParams(vmem_limit_bytes=48 << 20),
        name="solve",
    )(source, own_rows, *spread_parts[0], *spread_parts[1], windows, diag_inverse)

    spread_errors = spread(found)
    pruned = jnp.sum(jnp.where(mine[:, None, None], prune_mask, 0), 0).reshape(-1)
    flags = jnp.concatenate([(shift // TILE)[None], pruned]).astype(jnp.int32)
    split = pl.pallas_call(
        assemble_kernel,
        out_shape=jax.ShapeDtypeStruct((P_SIZE, rows, 3 * PW), jnp.bfloat16),
        in_specs=[smem] + [any_spec] * 8,
        out_specs=vmem,
        scratch_shapes=[
            pltpu.VMEM((2, rows, 3 * PW), jnp.float32),
            pltpu.SemaphoreType.DMA((64,)),
        ],
        compiler_params=pltpu.CompilerParams(vmem_limit_bytes=24 << 20),
        name="assemble",
    )(source, *spread_errors[0], *spread_errors[1])
    steps = pl.cdiv(width, NARROW)
    column = lambda i, *_: (0, i)
    return pl.pallas_call(
        update_kernel,
        out_shape=jax.ShapeDtypeStruct(weights.shape, jnp.float32),
        grid_spec=pltpu.PrefetchScalarGridSpec(
            num_scalar_prefetch=1,
            grid=(steps,),
            in_specs=[
                vmem,
                pl.BlockSpec((rows, NARROW), column),
                pl.BlockSpec((P_SIZE, PW, NARROW), lambda i, *_: (0, 0, i)),
            ],
            out_specs=pl.BlockSpec((rows, NARROW), column),
        ),
        compiler_params=pltpu.CompilerParams(vmem_limit_bytes=40 << 20),
        name="update",
    )(flags, split, weights, gathered)


def solution(mesh):
    torus = Mesh(
        mesh.devices.reshape(4, 4, 2, mesh.shape["row"]), ("col_0", "col_1", "col_2", "row")
    )
    return jax.shard_map(
        shards,
        mesh=torus,
        in_specs=(P("row", COL), P(None, "row", COL), P(), P(None, "row", None), P()),
        out_specs=P("row", COL),
        check_vma=False,
    )
```

```python
import functools

import jax
import jax.numpy as jnp
import numpy as np
from jax import lax
from jax.experimental import pallas as pl
from jax.experimental.pallas import tpu as pltpu
from jax.sharding import Mesh
from jax.sharding import PartitionSpec as P

TILE = 128
PANEL_TILES = 4
PW = 512
P_SIZE = 6
N_COL = 32
COL = ("col_0", "col_1", "col_2")
HOPS = ((0, 1), (1, 1), (0, 3), (1, 3))
BLOCKS = [(k, m) for k in range(P_SIZE) for m in range(k + 1)]
SLOTS = 6
HALF = SLOTS // 2
EARLY = 4
ROUND = 4
MINE = 16
NARROW = 256


def device(x, y, core):
    return (x * 4 + y) * 2 + core


def exchange(stream, stage):
    pairs = []
    for x in range(4):
        for y in range(4):
            for core in range(2):
                axis, bits = HOPS[(stream + stage + 2 * core) % 4]
                there = (x ^ bits, y) if axis == 0 else (x, y ^ bits)
                pairs.append((device(x, y, core), device(*there, core)))
    return pairs


def other_core(value):
    return lax.ppermute(value, "col_2", [(0, 1), (1, 0)])


def after(values, event):
    return list(lax.optimization_barrier((*values, event))[:-1])


def doubled(streams):
    near = [value[None] for value in streams]
    for stage in range(3):
        near = [
            jnp.concatenate([value, lax.ppermute(value, COL, exchange(i, stage))], 0)
            for i, value in enumerate(near)
        ]
    return near


def completed(near):
    far = [lax.ppermute(value, COL, exchange(i, 3)) for i, value in enumerate(near)]
    return [[near[i], far[i], other_core(near[i]), other_core(far[i])] for i in range(len(near))]


def all_rows(value):
    height = lax.axis_size("row")
    up = [(z, (z + 1) % height) for z in range(height)]
    down = [(z, (z - 1) % height) for z in range(height)]
    below, above = [value], [value]
    for hop in range(height // 2):
        below.append(lax.ppermute(below[-1], "row", up))
        if hop < height // 2 - 1:
            above.append(lax.ppermute(above[-1], "row", down))
    here = lax.axis_index("row")
    whole = jnp.zeros((value.shape[0], height, *value.shape[1:]), value.dtype)
    for i, part in enumerate(above + below[:0:-1]):
        place = lax.rem(here + i, height)
        whole = lax.dynamic_update_slice_in_dim(whole, part[:, None], place, 1)
    return whole


def sources():
    x, y, own = (lax.axis_index(name) for name in COL)
    steps = []
    for axis in range(2):
        value = np.zeros((2, 2, 16), np.int32)
        for core in range(2):
            for stream in range(2):
                for unit in range(16):
                    for stage in range(4):
                        hop, bits = HOPS[(stream + stage + 2 * core) % 4]
                        if hop == axis and unit >> stage & 1:
                            value[core, stream, unit] ^= bits
        steps.append(jnp.asarray(value))
    rows = []
    for core in (own, 1 - own):
        there_x = x ^ jnp.where(core == 0, steps[0][0], steps[0][1])
        there_y = y ^ jnp.where(core == 0, steps[1][0], steps[1][1])
        rows.append(device(there_x, there_y, core))
    return jnp.stack(rows, 1).astype(jnp.int32).reshape(-1)


def halves(value):
    high = value.astype(jnp.bfloat16)
    low = (value - high.astype(jnp.float32)).astype(jnp.bfloat16)
    return high, low


def product(left, right):
    dot = functools.partial(jnp.dot, preferred_element_type=jnp.float32)
    return dot(left[0], right[0]) + (dot(left[0], right[1]) + dot(left[1], right[0]))


def unit_copies(refs, place, semaphores):
    copies = []
    for stream in range(2):
        group = []
        for part in range(4):
            for unit in range(8):
                number = (stream * 2 + part // 2) * 16 + part % 2 * 8 + unit
                group.append(
                    pltpu.make_async_copy(
                        refs[stream * 4 + part].at[unit],
                        place(stream, number),
                        semaphores.at[number],
                    )
                )
        copies.append(group)
    return copies


def solve_kernel(early, source, flags, *refs):
    refs = list(refs)
    parts = [refs.pop(0) for _ in range(8)]
    windows, inverse = refs.pop(0), refs.pop(0)
    before = [] if early else [refs.pop(0) for _ in range(3)]
    outs = [refs.pop(0) for _ in range(3 if early else 2)]
    blocks, errors, semaphores = refs

    def place(stream, number):
        there = source[number]
        depth = pl.ds(stream * ROUND, ROUND)
        return blocks.at[:, there // 8, depth, lax.rem(there, 8)]

    copies = unit_copies(parts, place, semaphores)
    for group in copies:
        for copy in group:
            copy.start()
    for k in range(0 if early else EARLY):
        column = k % 2 * PW
        high, low = halves(before[k // 2][:, column : column + PW])
        errors[k, 0] = high
        errors[k, 1] = low
    for group in copies:
        for copy in group:
            copy.wait()

    def block_at(number):
        return halves(blocks[number // 4, lax.rem(number, 4)].reshape(PW, PW))

    def less(acc, base, first, last):
        def take(m, acc):
            return acc - product((errors[m, 0], errors[m, 1]), block_at(base + m))

        return lax.fori_loop(first, last, take, acc)

    skip = 0 if early else 4 * HALF
    for k in range(EARLY) if early else range(EARLY, P_SIZE):
        base = k * (k + 1) // 2 - skip
        if k == EARLY:
            window = less(before[2][...], base, -base, k)
        else:
            window = less(windows[k], base, 0, k)
        block = block_at(base + k)
        done = []
        for a in range(PANEL_TILES):
            tile = slice(a * TILE, (a + 1) * TILE)
            acc = window[:, tile]
            if a:
                left = tuple(jnp.concatenate([d[i] for d in done], 1) for i in range(2))
                acc = acc - product(left, tuple(b[: a * TILE, tile] for b in block))
            acc = product(halves(acc), halves(inverse[k, a]))
            acc = jnp.where(flags[k, a] != 0, acc, 0.0)
            done.append(halves(acc))
            stream, column = (k // 2, k % 2 * PW) if early else (k - EARLY, 0)
            outs[stream][:, column + a * TILE : column + (a + 1) * TILE] = acc
        for i in range(2):
            errors[k, i] = jnp.concatenate([d[i] for d in done], 1)
    if early:
        base = EARLY * (EARLY + 1) // 2
        outs[2][...] = less(windows[EARLY], base, 0, 4 * HALF - base)


def solve(early, source, flags, parts, windows, inverse, before):
    smem = pl.BlockSpec(memory_space=pltpu.SMEM)
    vmem = pl.BlockSpec(memory_space=pltpu.VMEM)
    widths = (2 * PW, 2 * PW, PW) if early else (PW, PW)
    return pl.pallas_call(
        functools.partial(solve_kernel, early),
        out_shape=[jax.ShapeDtypeStruct((MINE, width), jnp.float32) for width in widths],
        in_specs=[smem, smem]
        + [pl.BlockSpec(memory_space=pl.ANY)] * 8
        + [vmem] * (2 + len(before)),
        out_specs=[vmem] * len(widths),
        scratch_shapes=[
            pltpu.VMEM((HALF, 4, 8, 8, 8, PW), jnp.float32),
            pltpu.VMEM((P_SIZE, 2, MINE, PW), jnp.bfloat16),
            pltpu.SemaphoreType.DMA((64,)),
        ],
        compiler_params=pltpu.CompilerParams(vmem_limit_bytes=56 << 20),
        cost_estimate=pl.CostEstimate(
            flops=6_000_000_000, bytes_accessed=12 << 20, transcendentals=0
        ),
        name="solve_early" if early else "solve_late",
    )(source, flags, *parts[0], *parts[1], windows, inverse, *before)


def assemble_kernel(panels, source, *refs):
    parts, (out, errors, semaphores) = refs[:8], refs[8:]
    n = pl.program_id(0)

    def place(stream, number):
        first = pl.multiple_of(source[number] * MINE, MINE)
        return errors.at[stream, pl.ds(first, MINE)]

    @pl.when(n == 0)
    def _():
        copies = unit_copies(parts, place, semaphores)
        for group in copies:
            for copy in group:
                copy.start()
        for group in copies:
            for copy in group:
                copy.wait()

    column = pl.multiple_of(lax.rem(n, panels) * PW, PW)
    high, low = halves(errors[n // panels, :, pl.ds(column, PW)])
    out[0, :, :PW] = high
    out[0, :, PW : 2 * PW] = low
    out[0, :, 2 * PW :] = high


def assemble(panels, rows, source, parts):
    return pl.pallas_call(
        functools.partial(assemble_kernel, panels),
        out_shape=jax.ShapeDtypeStruct((2 * panels, rows, 3 * PW), jnp.bfloat16),
        grid_spec=pltpu.PrefetchScalarGridSpec(
            num_scalar_prefetch=1,
            grid=(2 * panels,),
            in_specs=[pl.BlockSpec(memory_space=pl.ANY)] * 8,
            out_specs=pl.BlockSpec((1, rows, 3 * PW), lambda i, *_: (i, 0, 0)),
            scratch_shapes=[
                pltpu.VMEM((2, rows, panels * PW), jnp.float32),
                pltpu.SemaphoreType.DMA((64,)),
            ],
        ),
        compiler_params=pltpu.CompilerParams(vmem_limit_bytes=56 << 20),
        cost_estimate=pl.CostEstimate(
            flops=20_000_000, bytes_accessed=panels << 22, transcendentals=0
        ),
        name=f"assemble_{panels}",
    )(source, *parts[0], *parts[1])


def update_kernel(flags, early, late, weights, factor, out):
    n = pl.program_id(0)
    out[...] = weights[...]

    def less(first, errors):
        def take(k, carry):
            high, low = halves(factor[first + k])
            rows = jnp.concatenate([high, high, low], 0)
            out[...] = out[...] - jnp.dot(errors[k], rows, preferred_element_type=jnp.float32)
            return carry

        lax.fori_loop(0, errors.shape[0], take, 0)

    less(0, early)
    less(EARLY, late)
    for part in range(NARROW // TILE):
        tile = n * (NARROW // TILE) + part - flags[0]
        inside = jnp.logical_and(tile >= 0, tile < PANEL_TILES)
        a = jnp.clip(tile, 0, PANEL_TILES - 1)
        columns = slice(part * TILE, (part + 1) * TILE)
        for r in range(4):
            gone = jnp.logical_and(inside, flags[1 + r * PANEL_TILES + a] != 0)

            @pl.when(gone)
            def _(r=r, columns=columns):
                out[r * TILE : (r + 1) * TILE, columns] = jnp.zeros((TILE, TILE), jnp.float32)


def shards(weights, factor, diag_inverse, prune_mask, panel_start):
    rows, width = weights.shape
    slab = factor.shape[1]
    me = lax.axis_index(COL)
    owner = panel_start // width
    mine = owner == me
    shift = jnp.sum(jnp.where(mine, panel_start - me * width, 0))
    panel = jnp.sum(jnp.where(mine, jnp.arange(P_SIZE, dtype=jnp.int32), 0))
    gathered = lax.all_gather(factor, "row", axis=1, tiled=True)

    window = lax.dynamic_slice(factor, (0, 0, shift), (P_SIZE, slab, PW))
    window = window.reshape(P_SIZE, 8, 8, PW)
    turn = lax.rem(panel * (panel + 1) // 2, 4)
    order = lax.rem(jnp.arange(4, dtype=jnp.int32) + 4 - turn, 4)
    order = jnp.minimum(order[:, None] + jnp.array([0, 4], jnp.int32), P_SIZE - 1)
    eighths = jnp.swapaxes(window[order], 1, 2).reshape(N_COL, 16, PW)
    wanted = lax.dynamic_slice(weights, (0, shift), (rows, PW)).reshape(N_COL, MINE, PW)
    arrived = lax.all_to_all(
        jnp.concatenate([eighths, wanted], 1), COL, 0, 0, tiled=True
    ).reshape(4 * N_COL, 8, PW)

    numbers = jnp.minimum(4 * jnp.arange(SLOTS, dtype=jnp.int32) + me // 8, len(BLOCKS) - 1)
    panels = jnp.array([k for k, _ in BLOCKS], jnp.int32)[numbers]
    parts = jnp.array([m // 4 for _, m in BLOCKS], jnp.int32)[numbers]
    picked = all_rows(arrived[owner[panels] * 4 + parts])
    windows = arrived[(owner[:, None] * 4 + jnp.array([2, 3], jnp.int32)).reshape(-1)]
    windows = windows.reshape(P_SIZE, MINE, PW)
    source = sources()
    own_rows = lax.dynamic_slice(prune_mask, (0, me // 8, 0), (P_SIZE, 1, PANEL_TILES))[:, 0]
    near = doubled([picked[:HALF, :ROUND], picked[:HALF, ROUND:]])
    late = after([picked[HALF:, :ROUND], picked[HALF:, ROUND:]], near[0][0, 0, 0, 0, :1])
    found = solve(True, source, own_rows, completed(near), windows, diag_inverse, [])
    near = after(doubled(late), found[0][0, :1])
    spread = completed(doubled(found[:2]))
    early = assemble(2, rows, source, spread)
    far = completed(near)
    event = spread[0][3][0, 0, :1]
    far = [after(parts[:3], event) + parts[3:] for parts in far]
    found = solve(False, source, own_rows, far, windows, diag_inverse, found)
    late = assemble(1, rows, source, completed(doubled(found)))

    pruned = jnp.sum(jnp.where(mine[:, None, None], prune_mask, 0), 0).reshape(-1)
    flags = jnp.concatenate([(shift // TILE)[None], pruned]).astype(jnp.int32)
    whole = lambda value: pl.BlockSpec(
        value.shape, lambda i, *_: (0, 0, 0), pipeline_mode=pl.Buffered(1)
    )
    steps = pl.cdiv(width, NARROW)
    column = lambda i, *_: (0, i)
    return pl.pallas_call(
        update_kernel,
        out_shape=jax.ShapeDtypeStruct(weights.shape, jnp.float32),
        grid_spec=pltpu.PrefetchScalarGridSpec(
            num_scalar_prefetch=1,
            grid=(steps,),
            in_specs=[
                whole(early),
                whole(late),
                pl.BlockSpec((rows, NARROW), column),
                pl.BlockSpec((P_SIZE, PW, NARROW), lambda i, *_: (0, 0, i)),
            ],
            out_specs=pl.BlockSpec((rows, NARROW), column),
        ),
        compiler_params=pltpu.CompilerParams(vmem_limit_bytes=56 << 20),
        name="update",
    )(flags, early, late, weights, gathered)


def solution(mesh):
    torus = Mesh(
        mesh.devices.reshape(4, 4, 2, mesh.shape["row"]), ("col_0", "col_1", "col_2", "row")
    )
    return jax.shard_map(
        shards,
        mesh=torus,
        in_specs=(P("row", COL), P(None, "row", COL), P(), P(None, "row", None), P()),
        out_specs=P("row", COL),
        check_vma=False,
    )
```

```python
import functools

import jax
import jax.numpy as jnp
import numpy as np
from jax import lax
from jax.experimental import pallas as pl
from jax.experimental.pallas import tpu as pltpu
from jax.sharding import Mesh
from jax.sharding import PartitionSpec as P

TILE = 128
PANEL_TILES = 4
PW = 512
P_SIZE = 6
N_COL = 32
COL = ("col_0", "col_1", "col_2")
HOPS = ((0, 1), (1, 1), (0, 3), (1, 3))
BLOCKS = [(k, m) for k in range(P_SIZE) for m in range(k + 1)]
EARLY = 10
MINE = 16
NARROW = 256


def device(x, y, core):
    return (x * 4 + y) * 2 + core


def exchange(stream, stage):
    pairs = []
    for x in range(4):
        for y in range(4):
            for core in range(2):
                axis, bits = HOPS[(stream + stage + 2 * core) % 4]
                there = (x ^ bits, y) if axis == 0 else (x, y ^ bits)
                pairs.append((device(x, y, core), device(*there, core)))
    return pairs


def other_core(value):
    return lax.ppermute(value, "col_2", [(0, 1), (1, 0)])


def spread(streams):
    every = []
    for i, value in enumerate(streams):
        value = value[None]
        for stage in range(2):
            value = jnp.concatenate([value, lax.ppermute(value, COL, exchange(i, stage))], 0)
        every.append([value])
    for stage in (2, 3):
        for i, parts in enumerate(every):
            parts += [lax.ppermute(part, COL, exchange(i, stage)) for part in parts]
    return [parts + [other_core(part) for part in parts] for parts in every]


def all_rows(value):
    height = lax.axis_size("row")
    up = [(z, (z + 1) % height) for z in range(height)]
    down = [(z, (z - 1) % height) for z in range(height)]
    below, above = [value], [value]
    for hop in range(height // 2):
        below.append(lax.ppermute(below[-1], "row", up))
        if hop < height // 2 - 1:
            above.append(lax.ppermute(above[-1], "row", down))
    here = lax.axis_index("row")
    whole = jnp.zeros((value.shape[0], height, *value.shape[1:]), value.dtype)
    for i, part in enumerate(above + below[:0:-1]):
        place = lax.rem(here + i, height)
        whole = lax.dynamic_update_slice_in_dim(whole, part[:, None], place, 1)
    return whole


def sources():
    x, y, own = (lax.axis_index(name) for name in COL)
    steps = []
    for axis in range(2):
        value = np.zeros((2, 2, 16), np.int32)
        for core in range(2):
            for stream in range(2):
                for unit in range(16):
                    for stage in range(4):
                        hop, bits = HOPS[(stream + stage + 2 * core) % 4]
                        if hop == axis and unit >> stage & 1:
                            value[core, stream, unit] ^= bits
        steps.append(jnp.asarray(value))
    rows = []
    for core in (own, 1 - own):
        there_x = x ^ jnp.where(core == 0, steps[0][0], steps[0][1])
        there_y = y ^ jnp.where(core == 0, steps[1][0], steps[1][1])
        rows.append(device(there_x, there_y, core))
    return jnp.stack(rows, 1).astype(jnp.int32).reshape(-1)


def halves(value):
    high = value.astype(jnp.bfloat16)
    low = (value - high.astype(jnp.float32)).astype(jnp.bfloat16)
    return high, low


def product(left, right):
    dot = functools.partial(jnp.dot, preferred_element_type=jnp.float32)
    return dot(left[0], right[0]) + (dot(left[0], right[1]) + dot(left[1], right[0]))


def unit_copies(refs, place, semaphores):
    copies = []
    for stream in range(2):
        group = []
        for part in range(8):
            for unit in range(4):
                number = stream * 32 + part * 4 + unit
                group.append(
                    pltpu.make_async_copy(
                        refs[stream * 8 + part].at[unit],
                        place(stream, number),
                        semaphores.at[number],
                    )
                )
        copies.append(group)
    return copies


def solve_kernel(source, flags, *refs):
    parts, (windows, inverse), outs = refs[:16], refs[16:18], refs[18:20]
    blocks, errors, semaphores = refs[20:]

    def place(stream, number):
        there = source[number]
        first, count = (0, EARLY) if stream == 0 else (EARLY, len(BLOCKS) - EARLY)
        column = pl.multiple_of(there // 8 * TILE, TILE)
        return blocks.at[pl.ds(first, count), :, lax.rem(there, 8), :, pl.ds(column, TILE)]

    copies = unit_copies(parts, place, semaphores)
    for group in copies:
        for copy in group:
            copy.start()
    for copy in copies[0]:
        copy.wait()

    def block_at(number):
        return halves(blocks[number].reshape(PW, PW))

    for k in range(P_SIZE):
        base = k * (k + 1) // 2
        if base == EARLY:
            for copy in copies[1]:
                copy.wait()

        def take(m, acc, base=base):
            return acc - product((errors[m, 0], errors[m, 1]), block_at(base + m))

        window = lax.fori_loop(0, k, take, windows[k])
        block = block_at(base + k)
        done = []
        for a in range(PANEL_TILES):
            tile = slice(a * TILE, (a + 1) * TILE)
            acc = window[:, tile]
            if a:
                left = tuple(jnp.concatenate([d[i] for d in done], 1) for i in range(2))
                acc = acc - product(left, tuple(b[: a * TILE, tile] for b in block))
            acc = product(halves(acc), halves(inverse[k, a]))
            acc = jnp.where(flags[k, a] != 0, acc, 0.0)
            done.append(halves(acc))
            column = (k % 3) * PW + a * TILE
            outs[k // 3][:, column : column + TILE] = acc
        for i in range(2):
            errors[k, i] = jnp.concatenate([d[i] for d in done], 1)


def update_kernel(source, flags, *refs):
    parts, (weights, factor, out), (errors, split, semaphores) = refs[:16], refs[16:19], refs[19:]
    n = pl.program_id(0)

    def place(stream, number):
        first = pl.multiple_of(source[number] * MINE, MINE)
        return errors.at[stream, pl.ds(first, MINE)]

    @pl.when(n == 0)
    def _():
        copies = unit_copies(parts, place, semaphores)
        for group in copies:
            for copy in group:
                copy.start()
        for group in copies:
            for copy in group:
                copy.wait()

        def divide(k, carry):
            column = pl.multiple_of(lax.rem(k, 3) * PW, PW)
            high, low = halves(errors[k // 3, :, pl.ds(column, PW)])
            split[k, :, :PW] = high
            split[k, :, PW : 2 * PW] = low
            split[k, :, 2 * PW :] = high
            return carry

        lax.fori_loop(0, P_SIZE, divide, 0)

    out[...] = weights[...]

    def take(k, carry):
        high, low = halves(factor[k])
        rows = jnp.concatenate([high, high, low], 0)
        out[...] = out[...] - jnp.dot(split[k], rows, preferred_element_type=jnp.float32)
        return carry

    lax.fori_loop(0, P_SIZE, take, 0)
    for part in range(NARROW // TILE):
        tile = n * (NARROW // TILE) + part - flags[0]
        inside = jnp.logical_and(tile >= 0, tile < PANEL_TILES)
        a = jnp.clip(tile, 0, PANEL_TILES - 1)
        columns = slice(part * TILE, (part + 1) * TILE)
        for r in range(4):
            gone = jnp.logical_and(inside, flags[1 + r * PANEL_TILES + a] != 0)

            @pl.when(gone)
            def _(r=r, columns=columns):
                out[r * TILE : (r + 1) * TILE, columns] = jnp.zeros((TILE, TILE), jnp.float32)


def shards(weights, factor, diag_inverse, prune_mask, panel_start):
    rows, width = weights.shape
    slab = factor.shape[1]
    me = lax.axis_index(COL)
    owner = panel_start // width
    mine = owner == me
    shift = jnp.sum(jnp.where(mine, panel_start - me * width, 0))
    panel = jnp.sum(jnp.where(mine, jnp.arange(P_SIZE, dtype=jnp.int32), 0))
    gathered = lax.all_gather(factor, "row", axis=1, tiled=True)

    window = lax.dynamic_slice(factor, (0, 0, shift), (P_SIZE, slab, PW))
    pieces = window.reshape(P_SIZE, 8, 8, 4, TILE).transpose(3, 1, 0, 2, 4)
    pieces = pieces.reshape(N_COL, P_SIZE, 8, TILE)
    wanted = lax.dynamic_slice(weights, (0, shift), (rows, PW))
    wanted = wanted.reshape(N_COL, 2, 8, 4, TILE).transpose(0, 1, 3, 2, 4)
    wanted = wanted.reshape(N_COL, 8, 8, TILE)
    arrived = lax.all_to_all(jnp.concatenate([pieces, wanted], 1), COL, 0, 0, tiled=True)

    each = arrived.shape[1]
    arrived = arrived.reshape(N_COL * each, 8, TILE)
    panels = np.array([k for k, _ in BLOCKS])
    rows_of = jnp.array([m for _, m in BLOCKS], jnp.int32)
    picked = all_rows(arrived[owner[panels] * each + rows_of])
    windows = arrived[(owner[:, None] * each + jnp.arange(P_SIZE, each)).reshape(-1)]
    windows = windows.reshape(P_SIZE, 2, 4, 8, TILE).transpose(0, 1, 3, 2, 4)
    windows = windows.reshape(P_SIZE, MINE, PW)
    source = sources()
    spread_parts = spread([picked[:EARLY], picked[EARLY:]])

    own_rows = lax.dynamic_slice(prune_mask, (0, me // 8, 0), (P_SIZE, 1, PANEL_TILES))[:, 0]
    any_spec = pl.BlockSpec(memory_space=pl.ANY)
    vmem = pl.BlockSpec(memory_space=pltpu.VMEM)
    smem = pl.BlockSpec(memory_space=pltpu.SMEM)
    found = pl.pallas_call(
        solve_kernel,
        out_shape=[jax.ShapeDtypeStruct((MINE, 3 * PW), jnp.float32)] * 2,
        in_specs=[smem, smem] + [any_spec] * 16 + [vmem, vmem],
        out_specs=[vmem, vmem],
        scratch_shapes=[
            pltpu.VMEM((len(BLOCKS), 8, 8, 8, PW), jnp.float32),
            pltpu.VMEM((P_SIZE, 2, MINE, PW), jnp.bfloat16),
            pltpu.SemaphoreType.DMA((64,)),
        ],
        compiler_params=pltpu.CompilerParams(vmem_limit_bytes=58 << 20),
        name="solve",
    )(source, own_rows, *spread_parts[0], *spread_parts[1], windows, diag_inverse)

    spread_errors = spread(found)
    pruned = jnp.sum(jnp.where(mine[:, None, None], prune_mask, 0), 0).reshape(-1)
    flags = jnp.concatenate([(shift // TILE)[None], pruned]).astype(jnp.int32)
    steps = pl.cdiv(width, NARROW)
    column = lambda i, *_: (0, i)
    return pl.pallas_call(
        update_kernel,
        out_shape=jax.ShapeDtypeStruct(weights.shape, jnp.float32),
        grid_spec=pltpu.PrefetchScalarGridSpec(
            num_scalar_prefetch=2,
            grid=(steps,),
            in_specs=[any_spec] * 16
            + [
                pl.BlockSpec((rows, NARROW), column),
                pl.BlockSpec((P_SIZE, PW, NARROW), lambda i, *_: (0, 0, i)),
            ],
            out_specs=pl.BlockSpec((rows, NARROW), column),
            scratch_shapes=[
                pltpu.VMEM((2, rows, 3 * PW), jnp.float32),
                pltpu.VMEM((P_SIZE, rows, 3 * PW), jnp.bfloat16),
                pltpu.SemaphoreType.DMA((64,)),
            ],
        ),
        compiler_params=pltpu.CompilerParams(vmem_limit_bytes=58 << 20),
        name="update",
    )(source, flags, *spread_errors[0], *spread_errors[1], weights, gathered)


def solution(mesh):
    torus = Mesh(
        mesh.devices.reshape(4, 4, 2, mesh.shape["row"]), ("col_0", "col_1", "col_2", "row")
    )
    return jax.shard_map(
        shards,
        mesh=torus,
        in_specs=(P("row", COL), P(None, "row", COL), P(), P(None, "row", None), P()),
        out_specs=P("row", COL),
        check_vma=False,
    )
```

```python
import functools

import jax
import jax.numpy as jnp
import numpy as np
from jax import lax
from jax.experimental import pallas as pl
from jax.experimental.pallas import tpu as pltpu
from jax.sharding import Mesh
from jax.sharding import PartitionSpec as P

TILE = 128
PANEL_TILES = 4
PW = 512
P_SIZE = 6
N_COL = 32
COL = ("col_0", "col_1", "col_2")
HOPS = ((0, 1), (1, 1), (0, 3), (1, 3))
BLOCKS = [(k, m) for k in range(P_SIZE) for m in range(k + 1)]
EARLY = 10
MINE = 16
NARROW = 256


def device(x, y, core):
    return (x * 4 + y) * 2 + core


def exchange(stream, stage):
    pairs = []
    for x in range(4):
        for y in range(4):
            for core in range(2):
                axis, bits = HOPS[(stream + stage + 2 * core) % 4]
                there = (x ^ bits, y) if axis == 0 else (x, y ^ bits)
                pairs.append((device(x, y, core), device(*there, core)))
    return pairs


def other_core(value):
    return lax.ppermute(value, "col_2", [(0, 1), (1, 0)])


def spread(streams, beside=()):
    every = []
    for i, value in enumerate(streams):
        value = value[None]
        for stage in range(2):
            value = jnp.concatenate([value, lax.ppermute(value, COL, exchange(i, stage))], 0)
        every.append([value])
    for stage in (2, 3):
        for i, parts in enumerate(every):
            parts += [lax.ppermute(part, COL, exchange(i, stage)) for part in parts]
            if beside and stage == 2 and i == 0:
                parts[1], *beside = lax.optimization_barrier((parts[1], *beside))
    return [parts + [other_core(part) for part in parts] for parts in every], beside


def all_rows(value):
    height = lax.axis_size("row")
    up = [(z, (z + 1) % height) for z in range(height)]
    down = [(z, (z - 1) % height) for z in range(height)]
    below, above = [value], [value]
    for hop in range(height // 2):
        below.append(lax.ppermute(below[-1], "row", up))
        if hop < height // 2 - 1:
            above.append(lax.ppermute(above[-1], "row", down))
    here = lax.axis_index("row")
    whole = jnp.zeros((value.shape[0], height, *value.shape[1:]), value.dtype)
    for i, part in enumerate(above + below[:0:-1]):
        place = lax.rem(here + i, height)
        whole = lax.dynamic_update_slice_in_dim(whole, part[:, None], place, 1)
    return whole


def sources():
    x, y, own = (lax.axis_index(name) for name in COL)
    steps = []
    for axis in range(2):
        value = np.zeros((2, 2, 16), np.int32)
        for core in range(2):
            for stream in range(2):
                for unit in range(16):
                    for stage in range(4):
                        hop, bits = HOPS[(stream + stage + 2 * core) % 4]
                        if hop == axis and unit >> stage & 1:
                            value[core, stream, unit] ^= bits
        steps.append(jnp.asarray(value))
    rows = []
    for core in (own, 1 - own):
        there_x = x ^ jnp.where(core == 0, steps[0][0], steps[0][1])
        there_y = y ^ jnp.where(core == 0, steps[1][0], steps[1][1])
        rows.append(device(there_x, there_y, core))
    return jnp.stack(rows, 1).astype(jnp.int32).reshape(-1)


def halves(value):
    high = value.astype(jnp.bfloat16)
    low = (value - high.astype(jnp.float32)).astype(jnp.bfloat16)
    return high, low


def product(left, right):
    dot = functools.partial(jnp.dot, preferred_element_type=jnp.float32)
    return dot(left[0], right[0]) + (dot(left[0], right[1]) + dot(left[1], right[0]))


def unit_copies(refs, place, semaphores):
    copies = []
    for stream in range(2):
        group = []
        for part in range(8):
            for unit in range(4):
                number = stream * 32 + part * 4 + unit
                group.append(
                    pltpu.make_async_copy(
                        refs[stream * 8 + part].at[unit],
                        place(stream, number),
                        semaphores.at[number],
                    )
                )
        copies.append(group)
    return copies


def solve_kernel(source, flags, *refs):
    parts, (windows, inverse), outs = refs[:16], refs[16:18], refs[18:20]
    blocks, errors, semaphores = refs[20:]

    def place(stream, number):
        there = source[number]
        first, count = (0, EARLY) if stream == 0 else (EARLY, len(BLOCKS) - EARLY)
        column = pl.multiple_of(there // 8 * TILE, TILE)
        return blocks.at[pl.ds(first, count), :, lax.rem(there, 8), :, pl.ds(column, TILE)]

    copies = unit_copies(parts, place, semaphores)
    for group in copies:
        for copy in group:
            copy.start()
    for copy in copies[0]:
        copy.wait()

    def block_at(number):
        return halves(blocks[number].reshape(PW, PW))

    for k in range(P_SIZE):
        base = k * (k + 1) // 2
        if base == EARLY:
            for copy in copies[1]:
                copy.wait()

        def take(m, acc, base=base):
            return acc - product((errors[m, 0], errors[m, 1]), block_at(base + m))

        window = lax.fori_loop(0, k, take, windows[k])
        block = block_at(base + k)
        done = []
        for a in range(PANEL_TILES):
            tile = slice(a * TILE, (a + 1) * TILE)
            acc = window[:, tile]
            if a:
                left = tuple(jnp.concatenate([d[i] for d in done], 1) for i in range(2))
                acc = acc - product(left, tuple(b[: a * TILE, tile] for b in block))
            acc = product(halves(acc), halves(inverse[k, a]))
            acc = jnp.where(flags[k, a] != 0, acc, 0.0)
            done.append(halves(acc))
            column = (k % 3) * PW + a * TILE
            outs[k // 3][:, column : column + TILE] = acc
        for i in range(2):
            errors[k, i] = jnp.concatenate([d[i] for d in done], 1)


def update_kernel(source, flags, *refs):
    parts, (weights, factor, out), (errors, split, semaphores) = refs[:16], refs[16:19], refs[19:]
    n = pl.program_id(0)

    def place(stream, number):
        first = pl.multiple_of(source[number] * MINE, MINE)
        return errors.at[stream, pl.ds(first, MINE)]

    @pl.when(n == 0)
    def _():
        copies = unit_copies(parts, place, semaphores)
        for group in copies:
            for copy in group:
                copy.start()
        for group in copies:
            for copy in group:
                copy.wait()

        def divide(k, carry):
            column = pl.multiple_of(lax.rem(k, 3) * PW, PW)
            high, low = halves(errors[k // 3, :, pl.ds(column, PW)])
            split[k, :, :PW] = high
            split[k, :, PW : 2 * PW] = low
            split[k, :, 2 * PW :] = high
            return carry

        lax.fori_loop(0, P_SIZE, divide, 0)

    total = weights[...]
    for k in range(P_SIZE):
        high, low = halves(factor[k])
        rows = jnp.concatenate([high, high, low], 0)
        total = total - jnp.dot(split[k], rows, preferred_element_type=jnp.float32)
    out[...] = total
    for part in range(NARROW // TILE):
        tile = n * (NARROW // TILE) + part - flags[0]
        inside = jnp.logical_and(tile >= 0, tile < PANEL_TILES)
        a = jnp.clip(tile, 0, PANEL_TILES - 1)
        columns = slice(part * TILE, (part + 1) * TILE)
        for r in range(4):
            gone = jnp.logical_and(inside, flags[1 + r * PANEL_TILES + a] != 0)

            @pl.when(gone)
            def _(r=r, columns=columns):
                out[r * TILE : (r + 1) * TILE, columns] = jnp.zeros((TILE, TILE), jnp.float32)


def shards(weights, factor, diag_inverse, prune_mask, panel_start):
    rows, width = weights.shape
    slab = factor.shape[1]
    me = lax.axis_index(COL)
    owner = panel_start // width
    mine = owner == me
    shift = jnp.sum(jnp.where(mine, panel_start - me * width, 0))
    panel = jnp.sum(jnp.where(mine, jnp.arange(P_SIZE, dtype=jnp.int32), 0))
    gathered = lax.all_gather(factor, "row", axis=1, tiled=True)

    window = lax.dynamic_slice(factor, (0, 0, shift), (P_SIZE, slab, PW))
    pieces = window.reshape(P_SIZE, 8, 8, 4, TILE).transpose(3, 1, 0, 2, 4)
    pieces = pieces.reshape(N_COL, P_SIZE, 8, TILE)
    wanted = lax.dynamic_slice(weights, (0, shift), (rows, PW))
    wanted = wanted.reshape(N_COL, 2, 8, 4, TILE).transpose(0, 1, 3, 2, 4)
    wanted = wanted.reshape(N_COL, 8, 8, TILE)
    arrived = lax.all_to_all(jnp.concatenate([pieces, wanted], 1), COL, 0, 0, tiled=True)

    each = arrived.shape[1]
    arrived = arrived.reshape(N_COL * each, 8, TILE)
    panels = np.array([k for k, _ in BLOCKS])
    rows_of = jnp.array([m for _, m in BLOCKS], jnp.int32)
    picked = all_rows(arrived[owner[panels] * each + rows_of])
    windows = arrived[(owner[:, None] * each + jnp.arange(P_SIZE, each)).reshape(-1)]
    windows = windows.reshape(P_SIZE, 2, 4, 8, TILE).transpose(0, 1, 3, 2, 4)
    windows = windows.reshape(P_SIZE, MINE, PW)
    source = sources()

    own_rows = lax.dynamic_slice(prune_mask, (0, me // 8, 0), (P_SIZE, 1, PANEL_TILES))[:, 0]
    pruned = jnp.sum(jnp.where(mine[:, None, None], prune_mask, 0), 0).reshape(-1)
    flags = jnp.concatenate([(shift // TILE)[None], pruned]).astype(jnp.int32)
    spread_parts, (windows, source, own_rows, flags) = spread(
        [picked[:EARLY], picked[EARLY:]], (windows, source, own_rows, flags)
    )
    any_spec = pl.BlockSpec(memory_space=pl.ANY)
    vmem = pl.BlockSpec(memory_space=pltpu.VMEM)
    smem = pl.BlockSpec(memory_space=pltpu.SMEM)
    found = pl.pallas_call(
        solve_kernel,
        out_shape=[jax.ShapeDtypeStruct((MINE, 3 * PW), jnp.float32)] * 2,
        in_specs=[smem, smem] + [any_spec] * 16 + [vmem, vmem],
        out_specs=[vmem, vmem],
        scratch_shapes=[
            pltpu.VMEM((len(BLOCKS), 8, 8, 8, PW), jnp.float32),
            pltpu.VMEM((P_SIZE, 2, MINE, PW), jnp.bfloat16),
            pltpu.SemaphoreType.DMA((64,)),
        ],
        compiler_params=pltpu.CompilerParams(vmem_limit_bytes=58 << 20),
        name="solve",
    )(source, own_rows, *spread_parts[0], *spread_parts[1], windows, diag_inverse)

    spread_errors, _ = spread(found)
    steps = pl.cdiv(width, NARROW)
    column = lambda i, *_: (0, i)
    return pl.pallas_call(
        update_kernel,
        out_shape=jax.ShapeDtypeStruct(weights.shape, jnp.float32),
        grid_spec=pltpu.PrefetchScalarGridSpec(
            num_scalar_prefetch=2,
            grid=(steps,),
            in_specs=[any_spec] * 16
            + [
                pl.BlockSpec((rows, NARROW), column),
                pl.BlockSpec((P_SIZE, PW, NARROW), lambda i, *_: (0, 0, i)),
            ],
            out_specs=pl.BlockSpec((rows, NARROW), column),
            scratch_shapes=[
                pltpu.VMEM((2, rows, 3 * PW), jnp.float32),
                pltpu.VMEM((P_SIZE, rows, 3 * PW), jnp.bfloat16),
                pltpu.SemaphoreType.DMA((64,)),
            ],
        ),
        compiler_params=pltpu.CompilerParams(vmem_limit_bytes=58 << 20),
        name="update",
    )(source, flags, *spread_errors[0], *spread_errors[1], weights, gathered)


def solution(mesh):
    torus = Mesh(
        mesh.devices.reshape(4, 4, 2, mesh.shape["row"]), ("col_0", "col_1", "col_2", "row")
    )
    return jax.shard_map(
        shards,
        mesh=torus,
        in_specs=(P("row", COL), P(None, "row", COL), P(), P(None, "row", None), P()),
        out_specs=P("row", COL),
        check_vma=False,
    )
```
